32 devices in a mesh: layer: 2 (over x), row: 4 (over z), col: 4 (over y, core).
Axes of the slice: x: 2, y: 2, z: 4, core: 2. Of those that a mesh axis runs over, the one named last changes fastest.
Arguments:
- query_weight: bfloat16 [32768, 16384], P(('layer', 'row'), 'col'), parts along dimension 0, may hold values from -0.046875 to 0.046875
- sign_input: int32 [32768], P(('layer', 'col')), parts along dimension 0, may hold values from -1 to 1, as said below
- sign_output: int32 [32768], P(('layer', 'row')), parts along dimension 0, may hold values from -1 to 1, as said below
- clip_level: int32 [256, 128], P(('layer', 'row'), 'col'), parts along dimension 0, may hold values from 1 to 8
- calibration: bfloat16 [768, 16384], P(('layer', 'row'), 'col'), parts along dimension 0, may hold values from -6 to 6
Outputs:
- projected: bfloat16 [768, 16384], P(('layer', 'col'), 'row'), parts along dimension 0
The draws below stay inside these ranges and needn't reach their ends.
There are 2 independent parts, one for each index of `layer`. The reference program is written for one: setup_inputs(seed, part) draws one part's arguments, and reference() takes and returns one part's arrays. A program takes and returns all parts, laid end to end along the dimension named above; each array names one. Nothing has to cross between parts.
Inputs may be any that keep to these rules, and one draw needn't show every extreme that they name: `sign_input`: every entry is -1 or 1. `sign_output`: every entry is -1 or 1.
All inputs are finite; a program needn't handle non-finite values.
Results may differ from the reference program's by a relative error of at most 0.0064.
Values may be sent and summed in bfloat16 or wider, within the bound.
A program may use at most 256 MiB of HBM per device.

```python
import jax
import jax.numpy as jnp
from jax import lax

OUTER = 16
INNER = 1024
D = 16384
BLK = 128
CAL = 384


def draw_sign_input(key, part):
    coin_flips = jax.random.randint(jax.random.fold_in(key, 11), (D,), 0, 2)
    return (2 * coin_flips - 1).astype(jnp.int32)


def draw_sign_output(key, part):
    coin_flips = jax.random.randint(jax.random.fold_in(key, 12), (D,), 0, 2)
    return (2 * coin_flips - 1).astype(jnp.int32)


def set_ends(result, own_key, low, high):
    longest = result.shape.index(max(result.shape))
    spots = []
    for shift in (0, 1):
        where = [jax.random.randint(jax.random.fold_in(own_key, axis), (), 0, length) for axis, length in enumerate(result.shape)]
        where[longest] = (where[longest] + shift) % result.shape[longest]
        spots.append(tuple(where))
    return result.at[spots[0]].set(low).at[spots[1]].set(high)


def steps_of(own_key, shape, cuts, least, largest):
    level = 1.0
    for axis_at, parts in cuts:
        steps = jax.random.uniform(jax.random.fold_in(jax.random.fold_in(own_key, 6), axis_at), (parts,), jnp.float32, least / len(cuts), largest / len(cuts))
        level = level * jnp.repeat(jnp.exp(steps), shape[axis_at] // parts).reshape((-1,) + (1,) * (len(shape) - 1 - axis_at))
    return level


def centred(own_key, dims, scale, reach, shards=(), held_as=jnp.bfloat16):
    array = jax.random.normal(own_key, dims, jnp.float32) * scale
    if len(shards) > 0:
        array = steps_of(own_key, dims, shards, -0.22, 0.18) * array
    return jnp.clip(array, min=-reach, max=reach).astype(held_as)


def setup_inputs(seed: int = 0, part: int = 0) -> dict:
    key_list = jax.random.split(jax.random.key(seed), 6)
    part_splits = jax.random.split(jax.random.fold_in(key_list[5], part), 6)
    query_weight = centred(part_splits[0], (D, D), D ** -0.5, 0.046875, ((0, 4), (1, 4)))
    sign_input = draw_sign_input(jax.random.fold_in(jax.random.fold_in(key_list[5], part), 71), part)
    sign_output = draw_sign_output(jax.random.fold_in(jax.random.fold_in(key_list[5], part), 71), part)
    clip_level = set_ends(jax.random.randint(part_splits[3], (D // BLK, D // BLK), 1, 9), jax.random.fold_in(part_splits[3], 1), 1, 8).astype(jnp.int32)
    calibration = centred(part_splits[4], (CAL, D), 1.0, 6.0, ((0, 4), (1, 4)))
    return dict(query_weight=query_weight, sign_input=sign_input, sign_output=sign_output, clip_level=clip_level, calibration=calibration)


def sylvester(length):
    indices = jnp.arange(length, dtype=jnp.int32)
    common_bits = indices[:, None] & indices[None, :]
    parity_sum = jnp.zeros((length, length), jnp.int32)
    for bit_number in range(max(length.bit_length() - 1, 1)):
        parity_sum = parity_sum ^ ((common_bits >> bit_number) & 1)
    return (1 - 2 * parity_sum).astype(jnp.float32)


def inner_right(weights, sign_vector, inner_size):
    row_total, col_total = weights.shape
    groups = inner_size // 128
    lane_table = jnp.asarray(sylvester(128), jnp.float32)
    mixing = jnp.asarray(sylvester(groups), jnp.float32)
    signed = weights.astype(jnp.float32) * sign_vector.astype(jnp.float32)[None, :]
    shaped = signed.reshape(row_total, col_total // inner_size, groups, 128)
    partial_sum = jnp.einsum('rage,ef->ragf', shaped, lane_table, precision=lax.Precision.HIGHEST)
    mixed = jnp.einsum('gh,rahf->ragf', mixing, partial_sum, precision=lax.Precision.HIGHEST)
    return mixed.reshape(row_total, col_total).astype(jnp.bfloat16)


def inner_left(weights, sign_vector, inner_size):
    row_total, col_total = weights.shape
    groups = inner_size // 128
    lane_table = jnp.asarray(sylvester(128), jnp.float32)
    mixing = jnp.asarray(sylvester(groups), jnp.float32)
    signed = weights.astype(jnp.float32) * sign_vector.astype(jnp.float32)[:, None]
    shaped = signed.reshape(row_total // inner_size, groups, 128, col_total)
    partial_sum = jnp.einsum('ef,cgek->cgfk', lane_table, shaped, precision=lax.Precision.HIGHEST)
    mixed = jnp.einsum('gh,chfk->cgfk', mixing, partial_sum, precision=lax.Precision.HIGHEST)
    return mixed.reshape(row_total, col_total).astype(jnp.bfloat16)


def reference(query_weight, sign_input, sign_output, clip_level, calibration):
    def first_pass(packed):
        rows_block, sign_rows = packed
        right_done = inner_right(rows_block, sign_input, INNER)
        return inner_left(right_done, sign_rows, INNER)

    inner_both = lax.map(first_pass, (query_weight.reshape(OUTER, INNER, D), sign_output.reshape(OUTER, INNER)))
    outer_table = jnp.asarray(sylvester(OUTER), jnp.float32)
    levels = clip_level.astype(jnp.float32) / 512.0

    def second_pass(index):
        def accumulate(source, total):
            return total + outer_table[index, source] * inner_both[source].astype(jnp.float32)

        mixed_rows = lax.fori_loop(0, OUTER, accumulate, jnp.zeros((INNER, D), jnp.float32))
        shaped = mixed_rows.reshape(INNER, OUTER, INNER)
        rotated = jnp.einsum('ak,dkb->dab', outer_table, shaped, precision=lax.Precision.HIGHEST).reshape(INNER, D) / D
        limit_rows = lax.dynamic_slice_in_dim(levels, (index * (INNER // BLK)).astype(jnp.int32), INNER // BLK, 0)
        limit_full = jnp.repeat(jnp.repeat(limit_rows, BLK, 0), BLK, 1)
        clipped = jnp.clip(rotated, -limit_full, limit_full).astype(jnp.bfloat16)
        return lax.dot_general(calibration, clipped, (((1,), (1,)), ((), ())), preferred_element_type=jnp.float32)

    pieces = lax.map(second_pass, jnp.arange(OUTER, dtype=jnp.int32))
    return jnp.transpose(pieces, (1, 0, 2)).reshape(CAL, D).astype(jnp.bfloat16)
```

```python
import functools

import jax
import jax.numpy as jnp
from jax import lax
from jax.experimental import pallas as pl
from jax.experimental.pallas import tpu as pltpu
from jax.sharding import PartitionSpec as P

INNER = 1024
D = 16384
BLK = 128
LANES = 128


def sylvester_bf16(length):
    at = jnp.arange(length, dtype=jnp.int32)
    parity = lax.population_count(at[:, None] & at[None, :]) & 1
    return (1 - 2 * parity).astype(jnp.bfloat16)


def inner_kernel(pieces, piece_rows, step, w_ref, si_ref, so_ref, k_ref, out_ref, ws_ref, ks_ref):
    ws_ref[...] = (w_ref[...].astype(jnp.float32) * si_ref[...]).astype(jnp.bfloat16)
    ks_ref[...] = (k_ref[...].astype(jnp.float32) * so_ref[0]).astype(jnp.bfloat16)
    inner = ws_ref.shape[0]

    @pl.loop(0, inner // step)
    def _(n):
        cols = pl.ds(pl.multiple_of(n * step, step), step)
        right = jnp.dot(ws_ref[...], k_ref[:, cols], preferred_element_type=jnp.float32)
        both = jnp.dot(ks_ref[...], right.astype(jnp.bfloat16), preferred_element_type=jnp.float32)
        out_ref[:, 0, :, cols] = both.reshape(pieces, piece_rows, step).astype(jnp.bfloat16)


def inner_both(weight, signs_in, signs_out, table, block, pieces):
    inner = table.shape[0]
    out_blocks = weight.shape[0] // inner
    piece_rows = inner // pieces
    step = min(256, inner)
    return pl.pallas_call(
        functools.partial(inner_kernel, pieces, piece_rows, step),
        grid=(out_blocks,),
        in_specs=[
            pl.BlockSpec((inner, inner), lambda c: (c, block)),
            pl.BlockSpec((1, inner), lambda c: (0, block)),
            pl.BlockSpec((1, 1, inner), lambda c: (c, 0, 0)),
            pl.BlockSpec((inner, inner), lambda c: (0, 0)),
        ],
        out_specs=pl.BlockSpec((pieces, 1, piece_rows, inner), lambda c: (0, c, 0, 0)),
        out_shape=jax.ShapeDtypeStruct((pieces, out_blocks, piece_rows, inner), jnp.bfloat16),
        scratch_shapes=[pltpu.VMEM((inner, inner), jnp.bfloat16)] * 2,
        cost_estimate=pl.CostEstimate(
            flops=4 * out_blocks * inner**3, bytes_accessed=4 * out_blocks * inner**2, transcendentals=0
        ),
    )(weight, signs_in, signs_out, table)


def butterfly(values):
    values = list(values)
    half = 1
    while half < len(values):
        for at in range(len(values)):
            if not at & half:
                low, high = values[at], values[at + half]
                values[at], values[at + half] = low + high, low - high
        half *= 2
    return values


def outer_kernel(row_count, col_count, out_blocks, in_blocks, scale, level_ref, *refs):
    parts = refs[:in_blocks]
    cal_ref, out_ref, mix_ref, clip_ref = refs[in_blocks:]
    b_at, d_at = pl.program_id(0), pl.program_id(1)
    chunk = mix_ref.shape[-1]
    lane_steps = chunk // LANES
    outer_rows = row_count * out_blocks
    outer_cols = col_count * in_blocks
    lane_blocks = level_ref.shape[1] // outer_cols

    @pl.loop(0, col_count * lane_steps)
    def _(at):
        q, lane = at // lane_steps, lax.rem(at, lane_steps)
        cols = pl.ds(pl.multiple_of(lane * LANES, LANES), LANES)
        for k in range(in_blocks):
            mixed = butterfly(
                parts[k][t * col_count + q, j, :, cols].astype(jnp.float32)
                for t in range(row_count)
                for j in range(out_blocks)
            )
            for o in range(outer_rows):
                mix_ref[q * in_blocks + k, o, :, cols] = mixed[o]

    @pl.loop(0, outer_rows * lane_steps)
    def _(at):
        o, lane = at // lane_steps, lax.rem(at, lane_steps)
        cols = pl.ds(pl.multiple_of(lane * LANES, LANES), LANES)
        mixed = butterfly(mix_ref[i, o, :, cols] for i in range(outer_cols))
        for i in range(outer_cols):
            level = level_ref[o, i * lane_blocks + b_at * lane_steps + lane]
            limit = level.astype(jnp.float32) / 512.0
            rotated = mixed[i] * scale
            clip_ref[i, o, :, cols] = jnp.minimum(jnp.maximum(rotated, -limit), limit).astype(jnp.bfloat16)

    total = None
    rows = clip_ref.shape[1] * clip_ref.shape[2]
    for q in range(col_count):
        for k in range(in_blocks):
            cal = cal_ref[:, q, k]
            cal = cal.reshape(cal.shape[0] * cal.shape[1], chunk)
            term = lax.dot_general(
                cal,
                clip_ref[q * in_blocks + k].reshape(rows, chunk),
                (((1,), (1,)), ((), ())),
                preferred_element_type=jnp.float32,
            )
            total = term if total is None else total + term

    @pl.when(b_at == 0)
    def _():
        out_ref[d_at] = total

    @pl.when(b_at > 0)
    def _():
        out_ref[d_at] += total


def outer_project(parts, level, cal, row_count, col_count, scale):
    in_blocks = len(parts)
    pieces, out_blocks, piece_rows, inner = parts[0].shape
    d_block = min(16, piece_rows)
    chunk = min(256, inner)
    outer_rows, outer_cols = row_count * out_blocks, col_count * in_blocks
    cal_local = cal.shape[3]
    cal_rows = row_count * cal_local
    d_steps = piece_rows // d_block
    return pl.pallas_call(
        functools.partial(outer_kernel, row_count, col_count, out_blocks, in_blocks, scale),
        grid=(inner // chunk, d_steps),
        in_specs=[pl.BlockSpec(memory_space=pltpu.SMEM)]
        + [pl.BlockSpec((pieces, out_blocks, d_block, chunk), lambda b, d: (0, 0, d, b))] * in_blocks
        + [pl.BlockSpec((row_count, col_count, in_blocks, cal_local, chunk), lambda b, d: (0, 0, 0, 0, b))],
        out_specs=pl.BlockSpec((d_steps, cal_rows, outer_rows * d_block), lambda b, d: (0, 0, 0)),
        out_shape=jax.ShapeDtypeStruct((d_steps, cal_rows, outer_rows * d_block), jnp.float32),
        scratch_shapes=[
            pltpu.VMEM((outer_cols, outer_rows, d_block, chunk), jnp.float32),
            pltpu.VMEM((outer_cols, outer_rows, d_block, chunk), jnp.bfloat16),
        ],
    )(level, *parts, cal)


def shards(query_weight, sign_input, sign_output, clip_level, calibration):
    rows_local, cols_local = query_weight.shape
    row_count = lax.axis_size("row")
    col_count = lax.axis_size("col")
    pieces = row_count * col_count
    out_blocks = rows_local // INNER
    in_blocks = cols_local // INNER
    piece_rows = INNER // pieces
    cal_local = calibration.shape[0]
    axes = ("row", "col")

    cal = calibration.reshape(cal_local, in_blocks, INNER).transpose(1, 0, 2)
    cal = lax.all_gather(cal, axes, axis=0, tiled=False)
    cal = cal.reshape(row_count, col_count, in_blocks, cal_local, INNER)
    level = lax.all_gather(lax.all_gather(clip_level, "col", axis=1, tiled=True), "row", axis=0, tiled=True)
    place = lax.axis_index("row") * col_count + lax.axis_index("col")
    level = level.reshape(row_count * out_blocks, INNER // BLK, -1)
    level = lax.dynamic_index_in_dim(level, place * piece_rows // BLK, axis=1, keepdims=False)

    table = sylvester_bf16(INNER)
    signs_in = sign_input.astype(jnp.float32).reshape(1, cols_local)
    signs_out = sign_output.astype(jnp.float32).reshape(out_blocks, 1, INNER)
    parts = []
    for block in range(in_blocks):
        tile = inner_both(query_weight, signs_in, signs_out, table, block, pieces)
        parts.append(lax.all_to_all(tile, axes, split_axis=0, concat_axis=0, tiled=True))

    total = outer_project(parts, level, cal, row_count, col_count, 1.0 / D)
    d_steps, cal_rows = total.shape[:2]
    d_block = piece_rows // d_steps
    result = total.astype(jnp.bfloat16)
    result = result.reshape(d_steps, col_count, cal_rows // col_count, row_count, out_blocks, d_block)
    result = result.transpose(3, 1, 2, 4, 0, 5)
    result = result.reshape(pieces, cal_rows // col_count, out_blocks, piece_rows)
    result = lax.all_to_all(result, axes, split_axis=0, concat_axis=0, tiled=True)
    return result.transpose(1, 2, 0, 3).reshape(cal_rows // col_count, rows_local)


def solution(mesh):
    placed = (
        P(("layer", "row"), "col"),
        P(("layer", "col")),
        P(("layer", "row")),
        P(("layer", "row"), "col"),
        P(("layer", "row"), "col"),
    )
    return jax.shard_map(
        shards, mesh=mesh, in_specs=placed, out_specs=P(("layer", "col"), "row"), check_vma=False
    )
```
